32 devices in a mesh: groups: 2 (over y), tile: 4 (over z), vec: 4 (over x, core).
Axes of the slice: x: 2, y: 2, z: 4, core: 2. Of those that a mesh axis runs over, the one named last changes fastest.
Arguments:
- vectors: float32 [2, 256, 3, 8192], P(None, 'vec', None, ('groups', 'tile')), parts along dimension 3, may hold values from -6 to 6
- links: float32 [3, 2, 3, 3, 8192], P(None, None, None, None, ('groups', 'tile')), parts along dimension 4, may hold values from -2.5 to 2.5
- momenta: int32 [8, 3], replicated, may hold values from -2 to 2
- directions: int32 [2], replicated, may hold values from 0 to 5
Outputs:
- elementals: float32 [512, 2, 2, 8, 256], P(('groups', 'tile'), None, None, None, 'vec'), parts along dimension 0
The draws below stay inside these ranges and needn't reach their ends.
There are 2 independent parts, one for each index of `groups`. The reference program is written for one: setup_inputs(seed, part) draws one part's arguments, and reference() takes and returns one part's arrays. A program takes and returns all parts, laid end to end along the dimension named above; an argument that names none is the same for every part. Nothing has to cross between parts.
Inputs may be any that keep to these rules, and one draw needn't show every extreme that they name: directions 0, 1, 2 step forward along the first, second, third dimension; 3, 4, 5 step backward along them.
All inputs are finite; a program needn't handle non-finite values.
Results may differ from the reference program's by a relative error of at most 0.00012.
Values sent between devices are 32-bit elements; how exact they have to be, the bound alone decides.
A program may use at most 128 MiB of HBM per device.

```python
import math
import jax
import jax.numpy as jnp
from jax import lax

NV = 256
LY = 16
LZ = 32
ITERS = 4
NMOM = 8
NDISP = 2
LX = 8
NSITES = 4096


def set_ends(entries, stream_key, least, top_value):
    longest = entries.shape.index(max(entries.shape))
    spots = []
    for shift in (0, 1):
        where = [jax.random.randint(jax.random.fold_in(stream_key, axis), (), 0, length) for axis, length in enumerate(entries.shape)]
        where[longest] = (where[longest] + shift) % entries.shape[longest]
        spots.append(tuple(where))
    return entries.at[spots[0]].set(least).at[spots[1]].set(top_value)


def block_scale(key, shape, pieces, smallest, top_value):
    gain = 1.0
    for position, shards_of in pieces:
        steps = jax.random.uniform(jax.random.fold_in(jax.random.fold_in(key, 6), position), (shards_of,), jnp.float32, smallest / len(pieces), top_value / len(pieces))
        gain = gain * jnp.repeat(jnp.exp(steps), shape[position] // shards_of).reshape((-1,) + (1,) * (len(shape) - 1 - position))
    return gain


def noise(stream_key, shape, width, limit, split=(), kind=jnp.bfloat16):
    values = jax.random.normal(stream_key, shape, jnp.float32) * width
    if len(split) > 0:
        values = block_scale(stream_key, shape, split, -0.22, 0.18) * values
    return jnp.clip(values, min=-limit, max=limit).astype(kind)


def setup_inputs(seed: int = 0, part: int = 0) -> dict:
    seeds = jax.random.split(jax.random.key(seed), 5)
    part_keys = jax.random.split(jax.random.fold_in(seeds[4], part), 5)
    return {
        "vectors": noise(part_keys[0], (2, NV, 3, NSITES), 1.0, 6.0, ((1, 4), (3, 4)), jnp.float32),
        "links": noise(part_keys[1], (3, 2, 3, 3, NSITES), 6 ** -0.5, 2.5, ((4, 4),), jnp.float32),
        "momenta": set_ends(jax.random.randint(seeds[2], (NMOM, 3), -2, 3), jax.random.fold_in(seeds[2], 1), -2, 2).astype(jnp.int32),
        "directions": jax.random.randint(seeds[3], (NDISP,), 0, 6).astype(jnp.int32),
    }


hop_scale = 0.125

def link_apply(link_real, link_imag, field_real, field_imag, dagger):
    if dagger:
        link_real = jnp.swapaxes(link_real, 0, 1)
        link_imag = -jnp.swapaxes(link_imag, 0, 1)
    out_real = 0.0
    out_imag = 0.0
    for column in range(3):
        left_real = link_real[:, column][None]
        left_imag = link_imag[:, column][None]
        right_real = field_real[:, column][:, None]
        right_imag = field_imag[:, column][:, None]
        out_real = out_real + left_real * right_real - left_imag * right_imag
        out_imag = out_imag + left_real * right_imag + left_imag * right_real
    return (out_real, out_imag)

def hop_field(source, forward, backward):
    total_real = 0.0
    total_imag = 0.0
    for spatial in range(3):
        ahead = jnp.roll(source, -1, axis=3 + spatial)
        behind = jnp.roll(source, 1, axis=3 + spatial)
        ahead_real, ahead_imag = link_apply(forward[spatial][0], forward[spatial][1], ahead[0], ahead[1], False)
        behind_real, behind_imag = link_apply(backward[spatial][0], backward[spatial][1], behind[0], behind[1], True)
        total_real = total_real + ahead_real + behind_real
        total_imag = total_imag + ahead_imag + behind_imag
    return hop_scale * jnp.stack([total_real, total_imag])

def phases(momenta, flat_index, extent_x):
    plane_size = LY * LZ
    coord_x = flat_index // plane_size
    coord_y = flat_index % plane_size // LZ
    coord_z = flat_index % LZ
    part_x = jnp.mod(momenta[:, 0:1] * coord_x[None], extent_x).astype(jnp.float32) / extent_x
    part_y = jnp.mod(momenta[:, 1:2] * coord_y[None], LY).astype(jnp.float32) / LY
    part_z = jnp.mod(momenta[:, 2:3] * coord_z[None], LZ).astype(jnp.float32) / LZ
    angle = 2.0 * math.pi * (part_x + part_y + part_z)
    return (jnp.cos(angle), jnp.sin(angle))

def right_matrix(right_stack):
    disp_count = right_stack.shape[0]
    column_count = right_stack.shape[2]
    flat_real = right_stack[:, 0].reshape(disp_count, column_count, -1)
    flat_imag = right_stack[:, 1].reshape(disp_count, column_count, -1)
    real_side = jnp.concatenate([flat_real, flat_imag], axis=2)
    imag_side = jnp.concatenate([flat_imag, -flat_real], axis=2)
    return jnp.stack([real_side, imag_side], axis=1)

def twist_left(left_field, cos_row, sin_row):
    row_count = left_field.shape[1]
    twisted_real = cos_row * left_field[0] - sin_row * left_field[1]
    twisted_imag = cos_row * left_field[1] + sin_row * left_field[0]
    return jnp.concatenate([twisted_real.reshape(row_count, -1), twisted_imag.reshape(row_count, -1)], axis=1)

def elemental_each(left_field, right_mat, cosine, sine, norm_factor):

    def one_momentum(phase_pair):
        left_flat = twist_left(left_field, phase_pair[0], phase_pair[1])
        return jnp.einsum('ik,dcjk->idcj', left_flat, right_mat, precision=lax.Precision.HIGHEST)
    result = lax.map(one_momentum, (cosine, sine))
    return jnp.transpose(result, (1, 2, 3, 0, 4)) * norm_factor

def reference(vectors, links, momenta, directions):
    field = vectors.reshape(2, NV, 3, LX, LY, LZ)
    gauge = links.reshape(3, 2, 3, 3, LX, LY, LZ)
    forward = [gauge[spatial] for spatial in range(3)]
    backward = [jnp.roll(gauge[spatial], 1, axis=3 + spatial) for spatial in range(3)]
    previous = field
    current = hop_field(field, forward, backward)
    for order in range(ITERS - 1):
        following = 2.0 * hop_field(current, forward, backward) - previous
        previous, current = (current, following)
    filtered = current

    def make_branch(heading):
        spatial = heading % 3
        if heading < 3:

            def branch_fn():
                ahead = jnp.roll(filtered, -1, axis=3 + spatial)
                return jnp.stack(link_apply(forward[spatial][0], forward[spatial][1], ahead[0], ahead[1], False))
        else:

            def branch_fn():
                behind = jnp.roll(filtered, 1, axis=3 + spatial)
                return jnp.stack(link_apply(backward[spatial][0], backward[spatial][1], behind[0], behind[1], True))
        return branch_fn
    branches = [make_branch(heading) for heading in range(6)]
    displaced = [lax.switch(directions[disp_slot], branches) for disp_slot in range(NDISP)]
    right_stack = jnp.stack(displaced).reshape(NDISP, 2, NV, 3, NSITES)
    flat_index = jnp.arange(NSITES, dtype=jnp.int32)
    cosine, sine = phases(momenta, flat_index, LX)
    norm_factor = 1.0 / math.sqrt(3.0 * NSITES)
    right_mat = right_matrix(right_stack)
    return elemental_each(filtered.reshape(2, NV, 3, NSITES), right_mat, cosine, sine, norm_factor)
```

```python
import functools
import math

import jax
import jax.numpy as jnp
from jax import lax
from jax.experimental import pallas as pl
from jax.experimental.pallas import tpu as pltpu
from jax.sharding import PartitionSpec as P

LY = 16
LZ = 32
ITERS = 4
PLANE = LY * LZ
LANES = 128
PER_PLANE = PLANE // LANES
HOP_SCALE = 0.125
VMEM_LIMIT = 60 * 1024 * 1024


def lane_index(like):
    return lax.broadcasted_iota(jnp.int32, like.shape, len(like.shape) - 1)


def shift_z(value, step):
    axis = len(value.shape) - 1
    lane = lane_index(value) % LZ
    if step > 0:
        plain = pltpu.roll(value, LANES - 1, axis)
        wrapped = pltpu.roll(value, LZ - 1, axis)
        return jnp.where(lane == LZ - 1, wrapped, plain)
    plain = pltpu.roll(value, 1, axis)
    wrapped = pltpu.roll(value, LANES - LZ + 1, axis)
    return jnp.where(lane == 0, wrapped, plain)


def shift_y(value, other, step):
    axis = len(value.shape) - 1
    lane = lane_index(value)
    if step > 0:
        return pltpu.roll(jnp.where(lane < LZ, other, value), LANES - LZ, axis)
    return pltpu.roll(jnp.where(lane >= LANES - LZ, other, value), LZ, axis)


def in_plane(chunk, step):
    base = chunk // PER_PLANE * PER_PLANE
    return base + (chunk + step + PER_PLANE) % PER_PLANE


def link_row(links, chunk, spatial, part, row, column):
    index = (part * 3 + row) * 3 + column
    return links[chunk, spatial, index : index + 1, :]


def apply_link(links, chunk, spatial, dagger, field, total):
    for row in range(3):
        real, imag = total[row], total[3 + row]
        for column in range(3):
            a, b = (column, row) if dagger else (row, column)
            lr = link_row(links, chunk, spatial, 0, a, b)
            li = link_row(links, chunk, spatial, 1, a, b)
            vr, vi = field[column], field[3 + column]
            if dagger:
                dr = lr * vr + li * vi
                di = lr * vi - li * vr
            else:
                dr = lr * vr - li * vi
                di = lr * vi + li * vr
            real = dr if real is None else real + dr
            imag = di if imag is None else imag + di
        total[row], total[3 + row] = real, imag
    return total


def moved(read, chunk, spatial, step, ahead_x):
    if spatial == 0:
        return [read(ahead_x, comp) for comp in range(6)]
    if spatial == 1:
        other = in_plane(chunk, step)
        return [shift_y(read(chunk, comp), read(other, comp), step) for comp in range(6)]
    return [shift_z(read(chunk, comp), step) for comp in range(6)]


def filter_kernel(field_ref, links_ref, out_ref, back_ref, first, second):
    chunks = field_ref.shape[0]

    @pl.loop(0, chunks)
    def _(chunk):
        back_ref[chunk, 0] = links_ref[(chunk - PER_PLANE + chunks) % chunks, 0]
        back_ref[chunk, 1] = shift_y(
            links_ref[chunk, 1], links_ref[in_plane(chunk, -1), 1], -1
        )
        back_ref[chunk, 2] = shift_z(links_ref[chunk, 2], -1)

    def hop(source, previous, target):
        @pl.loop(0, chunks)
        def _(chunk):
            read = lambda at, comp: source[at, comp]
            total = [None] * 6
            for spatial in range(3):
                ahead = moved(read, chunk, spatial, 1, (chunk + PER_PLANE) % chunks)
                total = apply_link(links_ref, chunk, spatial, False, ahead, total)
                behind = moved(
                    read, chunk, spatial, -1, (chunk - PER_PLANE + chunks) % chunks
                )
                total = apply_link(back_ref, chunk, spatial, True, behind, total)
            for comp in range(6):
                if previous is None:
                    target[chunk, comp] = HOP_SCALE * total[comp]
                else:
                    target[chunk, comp] = (
                        2.0 * HOP_SCALE * total[comp] - previous[chunk, comp]
                    )

    hop(field_ref, None, first)
    older, newer = field_ref, first
    for order in range(ITERS - 1):
        target = out_ref if order == ITERS - 2 else (second if order % 2 == 0 else first)
        hop(newer, older, target)
        older, newer = newer, target


def split(value):
    high = value.astype(jnp.bfloat16)
    low = (value - high.astype(jnp.float32)).astype(jnp.bfloat16)
    return high, low


def contract_kernel(
    dirs_ref, rows_ref, cols_ref, links_ref, back_ref, cos_ref, sin_ref,
    out_ref, shifted, left_hi, left_lo, right_hi, right_lo,
):
    chunk = pl.program_id(0)
    disps = shifted.shape[0]
    columns = cols_ref.shape[2]
    row_count = rows_ref.shape[2]
    momenta = cos_ref.shape[1]
    read = lambda at, comp: cols_ref[at + PER_PLANE, comp]

    for disp in range(disps):
        for heading in range(6):
            @pl.when(dirs_ref[disp] == heading)
            def _(disp=disp, heading=heading):
                spatial = heading % 3
                step = 1 if heading < 3 else -1
                for block in range(0, columns, 16):
                    stop = min(columns, block + 16)
                    part = lambda at, comp: cols_ref[at + PER_PLANE, comp, block:stop, :]
                    source = moved(part, chunk, spatial, step, chunk + step * PER_PLANE)
                    table = links_ref if step > 0 else back_ref
                    total = apply_link(table, chunk, spatial, step < 0, source, [None] * 6)
                    for comp in range(6):
                        shifted[disp, comp, block:stop, :] = total[comp]

    for colour in range(3):
        real_at = pl.ds(2 * colour * LANES, LANES)
        imag_at = pl.ds((2 * colour + 1) * LANES, LANES)
        hi, lo = split(rows_ref[0, colour])
        hi_i, lo_i = split(rows_ref[0, 3 + colour])
        for half, store_r, store_i in ((left_hi, hi, hi_i), (left_lo, lo, lo_i)):
            half[0:row_count, real_at] = store_r
            half[0:row_count, imag_at] = store_i
            half[row_count : 2 * row_count, real_at] = -store_i
            half[row_count : 2 * row_count, imag_at] = store_r
        for disp in range(disps):
            dr = shifted[disp, colour]
            di = shifted[disp, 3 + colour]
            for p in range(momenta):
                c = cos_ref[0, p : p + 1, :]
                s = sin_ref[0, p : p + 1, :]
                at = pl.ds((p * disps + disp) * columns, columns)
                hi, lo = split(c * dr + s * di)
                right_hi[at, real_at] = hi
                right_lo[at, real_at] = lo
                hi, lo = split(c * di - s * dr)
                right_hi[at, imag_at] = hi
                right_lo[at, imag_at] = lo

    @pl.when(chunk == 0)
    def _():
        out_ref[...] = jnp.zeros_like(out_ref)

    dims = (((1,), (1,)), ((), ()))
    dot = functools.partial(
        lax.dot_general, dimension_numbers=dims, preferred_element_type=jnp.float32
    )
    width = min(256, right_hi.shape[0])

    @pl.loop(0, right_hi.shape[0] // width)
    def _(block):
        at = pl.ds(pl.multiple_of(block * width, width), width)
        rh, rl = right_hi[at, :], right_lo[at, :]
        out_ref[:, at] += (
            dot(left_hi[...], rl) + dot(left_lo[...], rh) + dot(left_hi[...], rh)
        )


def phases(momenta, flat_index, extent_x):
    coord_x = flat_index // PLANE
    coord_y = flat_index % PLANE // LZ
    coord_z = flat_index % LZ
    part_x = jnp.mod(momenta[:, 0:1] * coord_x[None], extent_x).astype(jnp.float32) / extent_x
    part_y = jnp.mod(momenta[:, 1:2] * coord_y[None], LY).astype(jnp.float32) / LY
    part_z = jnp.mod(momenta[:, 2:3] * coord_z[None], LZ).astype(jnp.float32) / LZ
    angle = 2.0 * math.pi * (part_x + part_y + part_z)
    return (jnp.cos(angle), jnp.sin(angle))


def local(vectors, links, momenta, directions):
    nv = vectors.shape[1]
    sites = vectors.shape[3]
    tiles = lax.axis_size("tile")
    disps = directions.shape[0]
    moms = momenta.shape[0]
    chunks = sites // LANES
    every = chunks * tiles
    share = nv // tiles
    norm = 1.0 / math.sqrt(3.0 * sites * tiles)
    me = lax.axis_index("tile")

    field = vectors.reshape(2, tiles, share, 3, chunks, LANES)
    field = field.transpose(1, 4, 0, 3, 2, 5).reshape(tiles, chunks, 6, share, LANES)
    field = lax.all_to_all(field, "tile", 0, 0)
    field = field.reshape(every, 6, share, LANES)
    own_links = links.reshape(3, 18, chunks, LANES).transpose(2, 0, 1, 3)
    all_links = lax.all_gather(own_links, "tile", axis=0, tiled=True)

    vmem = pl.BlockSpec(memory_space=pltpu.VMEM)
    filtered, back = pl.pallas_call(
        filter_kernel,
        out_shape=(
            jax.ShapeDtypeStruct(field.shape, jnp.float32),
            jax.ShapeDtypeStruct(all_links.shape, jnp.float32),
        ),
        in_specs=[vmem, vmem],
        out_specs=(vmem, vmem),
        scratch_shapes=[pltpu.VMEM(field.shape, jnp.float32)] * 2,
        compiler_params=pltpu.CompilerParams(vmem_limit_bytes=VMEM_LIMIT),
        name="filter",
    )(field, all_links)

    slabs = filtered.reshape(tiles, chunks, 6, share, LANES)
    before = jnp.roll(slabs[:, chunks - PER_PLANE :], 1, axis=0)
    after = jnp.roll(slabs[:, :PER_PLANE], -1, axis=0)
    slabs = jnp.concatenate([before, slabs, after], axis=1)
    slabs = lax.all_to_all(slabs, "tile", 0, 0)
    wide = chunks + 2 * PER_PLANE
    cols = slabs.transpose(1, 2, 0, 3, 4).reshape(wide, 6, nv, LANES)
    rows = lax.all_gather(
        cols[PER_PLANE : PER_PLANE + chunks], "vec", axis=2, tiled=True
    )
    row_count = rows.shape[2]
    own_back = lax.dynamic_slice_in_dim(back, me * chunks, chunks, 0)

    flat_index = me * sites + jnp.arange(sites, dtype=jnp.int32)
    cosine, sine = phases(momenta, flat_index, sites * tiles // PLANE)
    cosine = (cosine * norm).reshape(moms, chunks, LANES).transpose(1, 0, 2)
    sine = (sine * norm).reshape(moms, chunks, LANES).transpose(1, 0, 2)

    width = moms * disps * nv
    one = lambda shape: pl.BlockSpec((1,) + shape, lambda i: (i,) + (0,) * len(shape))
    depth = 6 * LANES
    partial = pl.pallas_call(
        contract_kernel,
        grid=(chunks,),
        out_shape=jax.ShapeDtypeStruct((2 * row_count, width), jnp.float32),
        in_specs=[
            pl.BlockSpec(memory_space=pltpu.SMEM),
            one((6, row_count, LANES)),
            vmem,
            vmem,
            vmem,
            one((moms, LANES)),
            one((moms, LANES)),
        ],
        out_specs=pl.BlockSpec((2 * row_count, width), lambda i: (0, 0)),
        scratch_shapes=[
            pltpu.VMEM((disps, 6, nv, LANES), jnp.float32),
            pltpu.VMEM((2 * row_count, depth), jnp.bfloat16),
            pltpu.VMEM((2 * row_count, depth), jnp.bfloat16),
            pltpu.VMEM((width, depth), jnp.bfloat16),
            pltpu.VMEM((width, depth), jnp.bfloat16),
        ],
        compiler_params=pltpu.CompilerParams(vmem_limit_bytes=VMEM_LIMIT),
        name="contract",
    )(directions, rows, cols, own_links, own_back, cosine, sine)

    partial = partial.reshape(2, row_count, width)
    mine = lax.psum_scatter(partial, "tile", scatter_dimension=1, tiled=True)
    mine = mine.reshape(2, row_count // tiles, moms, disps, nv)
    return mine.transpose(1, 3, 0, 2, 4)


def solution(mesh):
    return jax.shard_map(
        local,
        mesh=mesh,
        in_specs=(
            P(None, "vec", None, ("groups", "tile")),
            P(None, None, None, None, ("groups", "tile")),
            P(),
            P(),
        ),
        out_specs=P(("groups", "tile"), None, None, None, "vec"),
        check_vma=False,
    )
```

```python
import functools
import math

import jax
import jax.numpy as jnp
from jax import lax
from jax.experimental import pallas as pl
from jax.experimental.pallas import tpu as pltpu
from jax.sharding import PartitionSpec as P

LY = 16
LZ = 32
ITERS = 4
PLANE = LY * LZ
LANES = 128
PER_PLANE = PLANE // LANES
HOP_SCALE = 0.125
VMEM_LIMIT = 60 * 1024 * 1024


def lane_index(like):
    return lax.broadcasted_iota(jnp.int32, like.shape, len(like.shape) - 1)


def shift_z(value, step):
    axis = len(value.shape) - 1
    lane = lane_index(value) % LZ
    if step > 0:
        plain = pltpu.roll(value, LANES - 1, axis)
        wrapped = pltpu.roll(value, LZ - 1, axis)
        return jnp.where(lane == LZ - 1, wrapped, plain)
    plain = pltpu.roll(value, 1, axis)
    wrapped = pltpu.roll(value, LANES - LZ + 1, axis)
    return jnp.where(lane == 0, wrapped, plain)


def shift_y(value, other, step):
    axis = len(value.shape) - 1
    lane = lane_index(value)
    if step > 0:
        return pltpu.roll(jnp.where(lane < LZ, other, value), LANES - LZ, axis)
    return pltpu.roll(jnp.where(lane >= LANES - LZ, other, value), LZ, axis)


def in_plane(chunk, step):
    base = chunk // PER_PLANE * PER_PLANE
    return base + (chunk + step + PER_PLANE) % PER_PLANE


def link_row(links, chunk, spatial, part, row, column):
    index = (part * 3 + row) * 3 + column
    return links[chunk, spatial, index : index + 1, :]


def apply_link(links, chunk, spatial, dagger, field, total):
    for row in range(3):
        real, imag = total[row], total[3 + row]
        for column in range(3):
            a, b = (column, row) if dagger else (row, column)
            lr = link_row(links, chunk, spatial, 0, a, b)
            li = link_row(links, chunk, spatial, 1, a, b)
            vr, vi = field[column], field[3 + column]
            if dagger:
                dr = lr * vr + li * vi
                di = lr * vi - li * vr
            else:
                dr = lr * vr - li * vi
                di = lr * vi + li * vr
            real = dr if real is None else real + dr
            imag = di if imag is None else imag + di
        total[row], total[3 + row] = real, imag
    return total


def moved(read, chunk, spatial, step, ahead_x):
    if spatial == 0:
        return [read(ahead_x, comp) for comp in range(6)]
    if spatial == 1:
        other = in_plane(chunk, step)
        return [shift_y(read(chunk, comp), read(other, comp), step) for comp in range(6)]
    return [shift_z(read(chunk, comp), step) for comp in range(6)]


def filter_kernel(count, me_ref, *refs):
    pieces, refs = refs[:count], refs[count:]
    all_links = refs[0]
    outs, refs = refs[1 : 1 + count], refs[1 + count :]
    own_back, field, first, second, links, back = refs
    chunks = field.shape[0]
    slab = chunks // count
    start = me_ref[0] * slab

    for index in range(count):
        field[index * slab : (index + 1) * slab] = pieces[index][...]

    @pl.loop(0, chunks)
    def _(chunk):
        links[chunk] = all_links[(chunk + start) % chunks]

    @pl.loop(0, chunks)
    def _(chunk):
        back[chunk, 0] = links[(chunk - PER_PLANE + chunks) % chunks, 0]
        back[chunk, 1] = shift_y(links[chunk, 1], links[in_plane(chunk, -1), 1], -1)
        back[chunk, 2] = shift_z(links[chunk, 2], -1)

    own_back[...] = back[0:slab]

    def hop(source, previous, target):
        @pl.loop(0, chunks)
        def _(chunk):
            read = lambda at, comp: source[at, comp]
            total = [None] * 6
            for spatial in range(3):
                ahead = moved(read, chunk, spatial, 1, (chunk + PER_PLANE) % chunks)
                total = apply_link(links, chunk, spatial, False, ahead, total)
                behind = moved(
                    read, chunk, spatial, -1, (chunk - PER_PLANE + chunks) % chunks
                )
                total = apply_link(back, chunk, spatial, True, behind, total)
            for comp in range(6):
                if previous is None:
                    target[chunk, comp] = HOP_SCALE * total[comp]
                else:
                    target[chunk, comp] = (
                        2.0 * HOP_SCALE * total[comp] - previous[chunk, comp]
                    )

    buffers = [field, first, second]
    hop(field, None, first)
    for order in range(1, ITERS):
        hop(buffers[1], buffers[0], buffers[2])
        buffers = [buffers[1], buffers[2], buffers[0]]
    for index in range(count):
        outs[index][...] = buffers[1][index * slab : (index + 1) * slab]


def split(value):
    high = value.astype(jnp.bfloat16)
    low = (value - high.astype(jnp.float32)).astype(jnp.bfloat16)
    return high, low


def contract_kernel(groups, me_ref, dirs_ref, *refs):
    rows_refs, refs = refs[:groups], refs[groups:]
    cols_refs, refs = refs[:groups], refs[groups:]
    links_ref, back_ref, cos_ref, sin_ref, out_ref = refs[:5]
    staged, shifted, left_hi, left_lo, right_hi, right_lo = refs[5:]
    chunk = pl.program_id(0)
    disps = shifted.shape[0]
    columns = shifted.shape[2]
    row_count = staged.shape[1]
    momenta = cos_ref.shape[1]
    tiles = cols_refs[0].shape[0]
    size = cols_refs[0].shape[3]
    share = size * groups

    @pl.loop(0, tiles)
    def _(turn):
        home = (me_ref[0] - turn + tiles) % tiles * share
        for group in range(groups):
            rows_ref, cols_ref = rows_refs[group], cols_refs[group]
            at = pl.ds(pl.multiple_of(home + group * size, size), size)
            for piece in range(rows_ref.shape[0]):
                place = pl.multiple_of(home + piece * columns + group * size, size)
                for comp in range(6):
                    staged[comp, pl.ds(place, size), :] = rows_ref[piece, turn, 0, comp]
            part = lambda where, comp: cols_ref[turn, where + PER_PLANE, comp]
            for disp in range(disps):
                for heading in range(6):
                    @pl.when(dirs_ref[disp] == heading)
                    def _(disp=disp, heading=heading):
                        spatial = heading % 3
                        step = 1 if heading < 3 else -1
                        source = moved(part, chunk, spatial, step, chunk + step * PER_PLANE)
                        table = links_ref if step > 0 else back_ref
                        total = apply_link(table, chunk, spatial, step < 0, source, [None] * 6)
                        for comp in range(6):
                            shifted[disp, comp, at, :] = total[comp]

    for colour in range(3):
        real_at = pl.ds(2 * colour * LANES, LANES)
        imag_at = pl.ds((2 * colour + 1) * LANES, LANES)
        hi, lo = split(staged[colour])
        hi_i, lo_i = split(staged[3 + colour])
        for half, store_r, store_i in ((left_hi, hi, hi_i), (left_lo, lo, lo_i)):
            half[0:row_count, real_at] = store_r
            half[0:row_count, imag_at] = store_i
            half[row_count : 2 * row_count, real_at] = -store_i
            half[row_count : 2 * row_count, imag_at] = store_r
        for disp in range(disps):
            dr = shifted[disp, colour]
            di = shifted[disp, 3 + colour]
            for p in range(momenta):
                c = cos_ref[0, p : p + 1, :]
                s = sin_ref[0, p : p + 1, :]
                at = pl.ds((p * disps + disp) * columns, columns)
                hi, lo = split(c * dr + s * di)
                right_hi[at, real_at] = hi
                right_lo[at, real_at] = lo
                hi, lo = split(c * di - s * dr)
                right_hi[at, imag_at] = hi
                right_lo[at, imag_at] = lo

    @pl.when(chunk == 0)
    def _():
        out_ref[...] = jnp.zeros_like(out_ref)

    dims = (((1,), (1,)), ((), ()))
    dot = functools.partial(
        lax.dot_general, dimension_numbers=dims, preferred_element_type=jnp.float32
    )
    width = min(256, right_hi.shape[0])

    @pl.loop(0, right_hi.shape[0] // width)
    def _(block):
        at = pl.ds(pl.multiple_of(block * width, width), width)
        rh, rl = right_hi[at, :], right_lo[at, :]
        out_ref[:, at] += (
            dot(left_hi[...], rl) + dot(left_lo[...], rh) + dot(left_hi[...], rh)
        )


def phases(momenta, flat_index, extent_x):
    coord_x = flat_index // PLANE
    coord_y = flat_index % PLANE // LZ
    coord_z = flat_index % LZ
    part_x = jnp.mod(momenta[:, 0:1] * coord_x[None], extent_x).astype(jnp.float32) / extent_x
    part_y = jnp.mod(momenta[:, 1:2] * coord_y[None], LY).astype(jnp.float32) / LY
    part_z = jnp.mod(momenta[:, 2:3] * coord_z[None], LZ).astype(jnp.float32) / LZ
    angle = 2.0 * math.pi * (part_x + part_y + part_z)
    return (jnp.cos(angle), jnp.sin(angle))


def local(vectors, links, momenta, directions):
    nv = vectors.shape[1]
    sites = vectors.shape[3]
    tiles = lax.axis_size("tile")
    disps = directions.shape[0]
    moms = momenta.shape[0]
    chunks = sites // LANES
    every = chunks * tiles
    share = nv // tiles
    norm = 1.0 / math.sqrt(3.0 * sites * tiles)
    me = lax.axis_index("tile")
    here = me.reshape(1).astype(jnp.int32)
    size = 8 if share % 8 == 0 else share
    groups = share // size

    def passed(value, steps):
        if steps % tiles == 0:
            return value
        return lax.ppermute(value, "tile", [(i, (i + steps) % tiles) for i in range(tiles)])

    own_links = links.reshape(3, 18, chunks, LANES).transpose(2, 0, 1, 3)
    all_links = lax.all_gather(own_links, "tile", axis=0, tiled=True)
    field = vectors.reshape(2, tiles, groups, size, 3, chunks, LANES)
    field = field.transpose(2, 1, 5, 0, 4, 3, 6)
    field = field.reshape(groups, tiles, chunks, 6, size, LANES)

    vmem = pl.BlockSpec(memory_space=pltpu.VMEM)
    smem = pl.BlockSpec(memory_space=pltpu.SMEM)
    piece = jax.ShapeDtypeStruct((chunks, 6, size, LANES), jnp.float32)
    whole_field = pltpu.VMEM((every, 6, size, LANES), jnp.float32)
    whole_links = pltpu.VMEM(all_links.shape, jnp.float32)
    run_filter = pl.pallas_call(
        functools.partial(filter_kernel, tiles),
        out_shape=(piece,) * tiles + (jax.ShapeDtypeStruct(own_links.shape, jnp.float32),),
        in_specs=[smem] + [vmem] * (tiles + 1),
        out_specs=(vmem,) * (tiles + 1),
        scratch_shapes=[whole_field] * 3 + [whole_links] * 2,
        compiler_params=pltpu.CompilerParams(vmem_limit_bytes=VMEM_LIMIT),
        cost_estimate=pl.CostEstimate(
            flops=12 * 10**9, bytes_accessed=2 * 10**6, transcendentals=0
        ),
        name="filter",
    )
    rolled = jnp.stack(
        [lax.dynamic_index_in_dim(field, (me + turn) % tiles, 1, False) for turn in range(tiles)]
    )
    slabs, gathered, own_back = [], [], None
    received = [
        [passed(rolled[turn, group], turn) for turn in range(tiles)] for group in range(groups)
    ]
    for group in range(groups):
        ordered = [received[group][(tiles - turn) % tiles] for turn in range(tiles)]
        *done, own_back = run_filter(here, *ordered, all_links)
        back = jnp.stack([passed(done[turn], turn) for turn in range(tiles)])
        slabs.append(back)
        gathered.append(lax.all_gather(back, "vec", axis=0))
    wide = []
    for slab in slabs:
        before = passed(slab[:, chunks - PER_PLANE :], 1)
        after = passed(slab[:, :PER_PLANE], -1)
        wide.append((before, slab, after))
    for group, (before, slab, after) in enumerate(wide):
        before = jnp.roll(before, 1, axis=0)
        after = jnp.roll(after, -1, axis=0)
        wide[group] = jnp.concatenate([before, slab, after], axis=1)

    flat_index = me * sites + jnp.arange(sites, dtype=jnp.int32)
    cosine, sine = phases(momenta, flat_index, sites * tiles // PLANE)
    cosine = (cosine * norm).reshape(moms, chunks, LANES).transpose(1, 0, 2)
    sine = (sine * norm).reshape(moms, chunks, LANES).transpose(1, 0, 2)

    row_count = nv * lax.axis_size("vec")
    halves = 2
    some = moms // halves
    width = some * disps * nv
    depth = 6 * LANES
    one = lambda shape: pl.BlockSpec((1,) + shape, lambda i: (i,) + (0,) * len(shape))
    row_block = pl.BlockSpec(
        (row_count // nv, tiles, 1, 6, size, LANES), lambda i: (0, 0, i, 0, 0, 0)
    )
    parts = []
    for half in range(halves):
        pick = slice(half * some, (half + 1) * some)
        partial = pl.pallas_call(
            functools.partial(contract_kernel, groups),
            grid=(chunks,),
            out_shape=jax.ShapeDtypeStruct((2 * row_count, width), jnp.float32),
            in_specs=[smem, smem]
            + [row_block] * groups
            + [vmem] * groups
            + [vmem, vmem, one((some, LANES)), one((some, LANES))],
            out_specs=pl.BlockSpec((2 * row_count, width), lambda i: (0, 0)),
            scratch_shapes=[
                pltpu.VMEM((6, row_count, LANES), jnp.float32),
                pltpu.VMEM((disps, 6, nv, LANES), jnp.float32),
                pltpu.VMEM((2 * row_count, depth), jnp.bfloat16),
                pltpu.VMEM((2 * row_count, depth), jnp.bfloat16),
                pltpu.VMEM((width, depth), jnp.bfloat16),
                pltpu.VMEM((width, depth), jnp.bfloat16),
            ],
            compiler_params=pltpu.CompilerParams(vmem_limit_bytes=VMEM_LIMIT),
            cost_estimate=pl.CostEstimate(
                flops=20 * 10**9, bytes_accessed=12 * 10**6, transcendentals=0
            ),
            name="contract",
        )(here, directions, *gathered, *wide, own_links, own_back, cosine[:, pick], sine[:, pick])
        partial = partial.reshape(2, row_count, width)
        mine = lax.psum_scatter(partial, "tile", scatter_dimension=1, tiled=True)
        parts.append(mine.reshape(2, row_count // tiles, some, disps, nv))
    mine = jnp.concatenate(parts, axis=2)
    return mine.transpose(1, 3, 0, 2, 4)


def solution(mesh):
    return jax.shard_map(
        local,
        mesh=mesh,
        in_specs=(
            P(None, "vec", None, ("groups", "tile")),
            P(None, None, None, None, ("groups", "tile")),
            P(),
            P(),
        ),
        out_specs=P(("groups", "tile"), None, None, None, "vec"),
        check_vma=False,
    )
```

```python
import functools
import math

import jax
import jax.numpy as jnp
from jax import lax
from jax.experimental import pallas as pl
from jax.experimental.pallas import tpu as pltpu
from jax.sharding import PartitionSpec as P

LY = 16
LZ = 32
ITERS = 4
PLANE = LY * LZ
LANES = 128
PER_PLANE = PLANE // LANES
HOP_SCALE = 0.125
VMEM_LIMIT = 60 * 1024 * 1024


def lane_index(like):
    return lax.broadcasted_iota(jnp.int32, like.shape, len(like.shape) - 1)


def shift_z(value, step):
    axis = len(value.shape) - 1
    lane = lane_index(value) % LZ
    if step > 0:
        plain = pltpu.roll(value, LANES - 1, axis)
        wrapped = pltpu.roll(value, LZ - 1, axis)
        return jnp.where(lane == LZ - 1, wrapped, plain)
    plain = pltpu.roll(value, 1, axis)
    wrapped = pltpu.roll(value, LANES - LZ + 1, axis)
    return jnp.where(lane == 0, wrapped, plain)


def shift_y(value, other, step):
    axis = len(value.shape) - 1
    lane = lane_index(value)
    if step > 0:
        return pltpu.roll(jnp.where(lane < LZ, other, value), LANES - LZ, axis)
    return pltpu.roll(jnp.where(lane >= LANES - LZ, other, value), LZ, axis)


def in_plane(chunk, step):
    base = chunk // PER_PLANE * PER_PLANE
    return base + (chunk + step + PER_PLANE) % PER_PLANE


def link_row(links, chunk, spatial, part, row, column):
    index = (part * 3 + row) * 3 + column
    return links[chunk, spatial, index : index + 1, :]


def apply_link(links, chunk, spatial, dagger, field, total):
    for row in range(3):
        real, imag = total[row], total[3 + row]
        for column in range(3):
            a, b = (column, row) if dagger else (row, column)
            lr = link_row(links, chunk, spatial, 0, a, b)
            li = link_row(links, chunk, spatial, 1, a, b)
            vr, vi = field[column], field[3 + column]
            if dagger:
                dr = lr * vr + li * vi
                di = lr * vi - li * vr
            else:
                dr = lr * vr - li * vi
                di = lr * vi + li * vr
            real = dr if real is None else real + dr
            imag = di if imag is None else imag + di
        total[row], total[3 + row] = real, imag
    return total


def moved(read, chunk, spatial, step, ahead_x):
    if spatial == 0:
        return [read(ahead_x, comp) for comp in range(6)]
    if spatial == 1:
        other = in_plane(chunk, step)
        return [shift_y(read(chunk, comp), read(other, comp), step) for comp in range(6)]
    return [shift_z(read(chunk, comp), step) for comp in range(6)]


def filter_kernel(count, me_ref, *refs):
    pieces, refs = refs[:count], refs[count:]
    all_links = refs[0]
    outs, refs = refs[1 : 1 + count], refs[1 + count :]
    own_back, field, first, second, links, back = refs
    chunks = field.shape[0]
    slab = chunks // count
    start = me_ref[0] * slab

    for index in range(count):
        field[index * slab : (index + 1) * slab] = pieces[index][...]

    @pl.loop(0, chunks)
    def _(chunk):
        links[chunk] = all_links[(chunk + start) % chunks]

    @pl.loop(0, chunks)
    def _(chunk):
        back[chunk, 0] = links[(chunk - PER_PLANE + chunks) % chunks, 0]
        back[chunk, 1] = shift_y(links[chunk, 1], links[in_plane(chunk, -1), 1], -1)
        back[chunk, 2] = shift_z(links[chunk, 2], -1)

    own_back[...] = back[0:slab]

    def hop(source, previous, target):
        @pl.loop(0, chunks)
        def _(chunk):
            read = lambda at, comp: source[at, comp]
            total = [None] * 6
            for spatial in range(3):
                ahead = moved(read, chunk, spatial, 1, (chunk + PER_PLANE) % chunks)
                total = apply_link(links, chunk, spatial, False, ahead, total)
                behind = moved(
                    read, chunk, spatial, -1, (chunk - PER_PLANE + chunks) % chunks
                )
                total = apply_link(back, chunk, spatial, True, behind, total)
            for comp in range(6):
                if previous is None:
                    target[chunk, comp] = HOP_SCALE * total[comp]
                else:
                    target[chunk, comp] = (
                        2.0 * HOP_SCALE * total[comp] - previous[chunk, comp]
                    )

    buffers = [field, first, second]
    hop(field, None, first)
    for order in range(1, ITERS):
        hop(buffers[1], buffers[0], buffers[2])
        buffers = [buffers[1], buffers[2], buffers[0]]
    for index in range(count):
        outs[index][...] = buffers[1][index * slab : (index + 1) * slab]


def split(value):
    high = value.astype(jnp.bfloat16)
    low = (value - high.astype(jnp.float32)).astype(jnp.bfloat16)
    return high, low


def displace_kernel(me_ref, dirs_ref, cols_ref, links_ref, back_ref, out_ref):
    chunks, disps = out_ref.shape[0], out_ref.shape[1]
    tiles, size = cols_ref.shape[0], cols_ref.shape[3]
    unrolled = min(tiles, 4)
    for disp in range(disps):
        for heading in range(6):
            @pl.when(dirs_ref[disp] == heading)
            def _(disp=disp, heading=heading):
                spatial = heading % 3
                step = 1 if heading < 3 else -1
                table = links_ref if step > 0 else back_ref

                @pl.loop(0, chunks * (tiles // unrolled))
                def _(index):
                    chunk = index % chunks
                    results = []
                    for inner in range(unrolled):
                        turn = index // chunks * unrolled + inner
                        part = lambda where, comp: cols_ref[turn, where + PER_PLANE, comp]
                        source = moved(part, chunk, spatial, step, chunk + step * PER_PLANE)
                        total = apply_link(table, chunk, spatial, step < 0, source, [None] * 6)
                        results.append((turn, total))
                    for turn, total in results:
                        home = pl.multiple_of((me_ref[0] - turn + tiles) % tiles * size, size)
                        for comp in range(6):
                            out_ref[chunk, disp, comp, pl.ds(home, size), :] = total[comp]


def contract_kernel(me_ref, rows_ref, shifted_ref, cos_ref, sin_ref, out_ref, *scratch):
    staged, left_hi, left_lo, right_hi, right_lo = scratch
    shifted = shifted_ref.at[0]
    chunk = pl.program_id(0)
    disps = shifted_ref.shape[1]
    columns = shifted_ref.shape[3]
    row_count = staged.shape[1]
    momenta = cos_ref.shape[1]
    tiles, size = rows_ref.shape[1], rows_ref.shape[4]

    @pl.loop(0, tiles)
    def _(turn):
        home = (me_ref[0] - turn + tiles) % tiles * size
        for piece in range(rows_ref.shape[0]):
            place = pl.multiple_of(home + piece * columns, size)
            for comp in range(6):
                staged[comp, pl.ds(place, size), :] = rows_ref[piece, turn, 0, comp]

    for colour in range(3):
        real_at = pl.ds(2 * colour * LANES, LANES)
        imag_at = pl.ds((2 * colour + 1) * LANES, LANES)
        hi, lo = split(staged[colour])
        hi_i, lo_i = split(staged[3 + colour])
        for half, store_r, store_i in ((left_hi, hi, hi_i), (left_lo, lo, lo_i)):
            half[0:row_count, real_at] = store_r
            half[0:row_count, imag_at] = store_i
            half[row_count : 2 * row_count, real_at] = -store_i
            half[row_count : 2 * row_count, imag_at] = store_r
        for disp in range(disps):
            dr = shifted[disp, colour]
            di = shifted[disp, 3 + colour]
            for p in range(momenta):
                c = cos_ref[0, p : p + 1, :]
                s = sin_ref[0, p : p + 1, :]
                at = pl.ds((p * disps + disp) * columns, columns)
                hi, lo = split(c * dr + s * di)
                right_hi[at, real_at] = hi
                right_lo[at, real_at] = lo
                hi, lo = split(c * di - s * dr)
                right_hi[at, imag_at] = hi
                right_lo[at, imag_at] = lo

    @pl.when(chunk == 0)
    def _():
        out_ref[...] = jnp.zeros_like(out_ref)

    dims = (((1,), (1,)), ((), ()))
    dot = functools.partial(
        lax.dot_general, dimension_numbers=dims, preferred_element_type=jnp.float32
    )
    width = min(256, right_hi.shape[0])

    @pl.loop(0, right_hi.shape[0] // width)
    def _(block):
        at = pl.ds(pl.multiple_of(block * width, width), width)
        rh, rl = right_hi[at, :], right_lo[at, :]
        out_ref[:, at] += (
            dot(left_hi[...], rl) + dot(left_lo[...], rh) + dot(left_hi[...], rh)
        )


def phases(momenta, flat_index, extent_x):
    coord_x = flat_index // PLANE
    coord_y = flat_index % PLANE // LZ
    coord_z = flat_index % LZ
    part_x = jnp.mod(momenta[:, 0:1] * coord_x[None], extent_x).astype(jnp.float32) / extent_x
    part_y = jnp.mod(momenta[:, 1:2] * coord_y[None], LY).astype(jnp.float32) / LY
    part_z = jnp.mod(momenta[:, 2:3] * coord_z[None], LZ).astype(jnp.float32) / LZ
    angle = 2.0 * math.pi * (part_x + part_y + part_z)
    return (jnp.cos(angle), jnp.sin(angle))


def local(vectors, links, momenta, directions):
    nv = vectors.shape[1]
    sites = vectors.shape[3]
    tiles = lax.axis_size("tile")
    disps = directions.shape[0]
    moms = momenta.shape[0]
    chunks = sites // LANES
    every = chunks * tiles
    share = nv // tiles
    norm = 1.0 / math.sqrt(3.0 * sites * tiles)
    me = lax.axis_index("tile")
    here = me.reshape(1).astype(jnp.int32)
    groups, size = 1, share

    def passed(value, steps):
        if steps % tiles == 0:
            return value
        return lax.ppermute(value, "tile", [(i, (i + steps) % tiles) for i in range(tiles)])

    own_links = links.reshape(3, 18, chunks, LANES).transpose(2, 0, 1, 3)
    quarters = math.gcd(lax.axis_size("vec"), chunks)
    some_chunks = chunks // quarters
    mine_at = lax.axis_index("vec") % quarters * some_chunks
    quarter = lax.dynamic_slice_in_dim(own_links, mine_at, some_chunks, 0)
    quarter = lax.all_gather(quarter, "tile", axis=0)
    all_links = lax.all_gather(quarter, "vec", axis=0)[:quarters]
    all_links = all_links.transpose(1, 0, 2, 3, 4, 5).reshape(every, 3, 18, LANES)
    field = vectors.reshape(2, tiles, groups, size, 3, chunks, LANES)
    field = field.transpose(2, 1, 5, 0, 4, 3, 6)
    field = field.reshape(groups, tiles, chunks, 6, size, LANES)

    vmem = pl.BlockSpec(memory_space=pltpu.VMEM)
    smem = pl.BlockSpec(memory_space=pltpu.SMEM)
    piece = jax.ShapeDtypeStruct((chunks, 6, size, LANES), jnp.float32)
    whole_field = pltpu.VMEM((every, 6, size, LANES), jnp.float32)
    whole_links = pltpu.VMEM(all_links.shape, jnp.float32)
    run_filter = pl.pallas_call(
        functools.partial(filter_kernel, tiles),
        out_shape=(piece,) * tiles + (jax.ShapeDtypeStruct(own_links.shape, jnp.float32),),
        in_specs=[smem] + [vmem] * (tiles + 1),
        out_specs=(vmem,) * (tiles + 1),
        scratch_shapes=[whole_field] * 3 + [whole_links] * 2,
        compiler_params=pltpu.CompilerParams(vmem_limit_bytes=VMEM_LIMIT),
        cost_estimate=pl.CostEstimate(
            flops=12 * 10**9, bytes_accessed=2 * 10**6, transcendentals=0
        ),
        name="filter",
    )
    rolled = jnp.stack(
        [lax.dynamic_index_in_dim(field, (me + turn) % tiles, 1, False) for turn in range(tiles)]
    )
    slabs, gathered, own_back = [], [], None
    received = [
        [passed(rolled[turn, group], turn) for turn in range(tiles)] for group in range(groups)
    ]
    for group in range(groups):
        ordered = [received[group][(tiles - turn) % tiles] for turn in range(tiles)]
        *done, own_back = run_filter(here, *ordered, all_links)
        back = jnp.stack([passed(done[turn], turn) for turn in range(tiles)])
        slabs.append(back)
        gathered.append(lax.all_gather(back, "vec", axis=0))
    wide = []
    for slab in slabs:
        before = passed(slab[:, chunks - PER_PLANE :], 1)
        after = passed(slab[:, :PER_PLANE], -1)
        wide.append((before, slab, after))
    for group, (before, slab, after) in enumerate(wide):
        before = jnp.roll(before, 1, axis=0)
        after = jnp.roll(after, -1, axis=0)
        wide[group] = jnp.concatenate([before, slab, after], axis=1)

    flat_index = me * sites + jnp.arange(sites, dtype=jnp.int32)
    cosine, sine = phases(momenta, flat_index, sites * tiles // PLANE)
    cosine = (cosine * norm).reshape(moms, chunks, LANES).transpose(1, 0, 2)
    sine = (sine * norm).reshape(moms, chunks, LANES).transpose(1, 0, 2)

    row_count = nv * lax.axis_size("vec")
    halves = 2
    some = moms // halves
    width = some * disps * nv
    depth = 6 * LANES
    one = lambda shape: pl.BlockSpec((1,) + shape, lambda i: (i,) + (0,) * len(shape))
    row_block = pl.BlockSpec(
        (row_count // nv, tiles, 1, 6, size, LANES), lambda i: (0, 0, i, 0, 0, 0)
    )
    displaced = pl.pallas_call(
        displace_kernel,
        out_shape=jax.ShapeDtypeStruct((chunks, disps, 6, nv, LANES), jnp.float32),
        in_specs=[smem, smem, vmem, vmem, vmem],
        out_specs=vmem,
        compiler_params=pltpu.CompilerParams(vmem_limit_bytes=VMEM_LIMIT),
        name="displace",
    )(here, directions, wide[0], own_links, own_back)
    parts = []
    for half in range(halves):
        pick = slice(half * some, (half + 1) * some)
        partial = pl.pallas_call(
            contract_kernel,
            grid=(chunks,),
            out_shape=jax.ShapeDtypeStruct((2 * row_count, width), jnp.float32),
            in_specs=[
                smem,
                row_block,
                one((disps, 6, nv, LANES)),
                one((some, LANES)),
                one((some, LANES)),
            ],
            out_specs=pl.BlockSpec((2 * row_count, width), lambda i: (0, 0)),
            scratch_shapes=[
                pltpu.VMEM((6, row_count, LANES), jnp.float32),
                pltpu.VMEM((2 * row_count, depth), jnp.bfloat16),
                pltpu.VMEM((2 * row_count, depth), jnp.bfloat16),
                pltpu.VMEM((width, depth), jnp.bfloat16),
                pltpu.VMEM((width, depth), jnp.bfloat16),
            ],
            compiler_params=pltpu.CompilerParams(vmem_limit_bytes=VMEM_LIMIT),
            cost_estimate=pl.CostEstimate(
                flops=20 * 10**9, bytes_accessed=12 * 10**6, transcendentals=0
            ),
            name="contract",
        )(here, gathered[0], displaced, cosine[:, pick], sine[:, pick])
        partial = partial.reshape(2, row_count, width)
        mine = lax.psum_scatter(partial, "tile", scatter_dimension=1, tiled=True)
        parts.append(mine.reshape(2, row_count // tiles, some, disps, nv))
    mine = jnp.concatenate(parts, axis=2)
    return mine.transpose(1, 3, 0, 2, 4)


def solution(mesh):
    return jax.shard_map(
        local,
        mesh=mesh,
        in_specs=(
            P(None, "vec", None, ("groups", "tile")),
            P(None, None, None, None, ("groups", "tile")),
            P(),
            P(),
        ),
        out_specs=P(("groups", "tile"), None, None, None, "vec"),
        check_vma=False,
    )
```

```python
import functools
import math

import jax
import jax.numpy as jnp
from jax import lax
from jax.experimental import pallas as pl
from jax.experimental.pallas import tpu as pltpu
from jax.sharding import PartitionSpec as P

LY = 16
LZ = 32
ITERS = 4
PLANE = LY * LZ
LANES = 128
PER_PLANE = PLANE // LANES
HOP_SCALE = 0.125
VMEM_LIMIT = 60 * 1024 * 1024


def lane_index(like):
    return lax.broadcasted_iota(jnp.int32, like.shape, len(like.shape) - 1)


def shift_z(value, step):
    axis = len(value.shape) - 1
    lane = lane_index(value) % LZ
    if step > 0:
        plain = pltpu.roll(value, LANES - 1, axis)
        wrapped = pltpu.roll(value, LZ - 1, axis)
        return jnp.where(lane == LZ - 1, wrapped, plain)
    plain = pltpu.roll(value, 1, axis)
    wrapped = pltpu.roll(value, LANES - LZ + 1, axis)
    return jnp.where(lane == 0, wrapped, plain)


def shift_y(value, other, step):
    axis = len(value.shape) - 1
    lane = lane_index(value)
    if step > 0:
        return pltpu.roll(jnp.where(lane < LZ, other, value), LANES - LZ, axis)
    return pltpu.roll(jnp.where(lane >= LANES - LZ, other, value), LZ, axis)


def in_plane(chunk, step):
    base = chunk // PER_PLANE * PER_PLANE
    return base + (chunk + step + PER_PLANE) % PER_PLANE


def link_row(links, chunk, spatial, part, row, column):
    index = (part * 3 + row) * 3 + column
    return links[chunk, spatial, index : index + 1, :]


def apply_link(links, chunk, spatial, dagger, field, total):
    for row in range(3):
        real, imag = total[row], total[3 + row]
        for column in range(3):
            a, b = (column, row) if dagger else (row, column)
            lr = link_row(links, chunk, spatial, 0, a, b)
            li = link_row(links, chunk, spatial, 1, a, b)
            vr, vi = field[column], field[3 + column]
            if dagger:
                dr = lr * vr + li * vi
                di = lr * vi - li * vr
            else:
                dr = lr * vr - li * vi
                di = lr * vi + li * vr
            real = dr if real is None else real + dr
            imag = di if imag is None else imag + di
        total[row], total[3 + row] = real, imag
    return total


def moved(read, chunk, spatial, step, ahead_x):
    if spatial == 0:
        return [read(ahead_x, comp) for comp in range(6)]
    if spatial == 1:
        other = in_plane(chunk, step)
        return [shift_y(read(chunk, comp), read(other, comp), step) for comp in range(6)]
    return [shift_z(read(chunk, comp), step) for comp in range(6)]


def filter_kernel(count, me_ref, *refs):
    pieces, refs = refs[:count], refs[count:]
    all_links = refs[0]
    outs, refs = refs[1 : 1 + count], refs[1 + count :]
    own_back, field, first, second, links, back = refs
    chunks = field.shape[0]
    slab = chunks // count
    start = me_ref[0] * slab

    for index in range(count):
        field[index * slab : (index + 1) * slab] = pieces[index][...]

    @pl.loop(0, chunks)
    def _(chunk):
        links[chunk] = all_links[(chunk + start) % chunks]

    @pl.loop(0, chunks)
    def _(chunk):
        back[chunk, 0] = links[(chunk - PER_PLANE + chunks) % chunks, 0]
        back[chunk, 1] = shift_y(links[chunk, 1], links[in_plane(chunk, -1), 1], -1)
        back[chunk, 2] = shift_z(links[chunk, 2], -1)

    own_back[...] = back[0:slab]

    def hop(source, previous, target):
        @pl.loop(0, chunks)
        def _(chunk):
            read = lambda at, comp: source[at, comp]
            total = [None] * 6
            for spatial in range(3):
                ahead = moved(read, chunk, spatial, 1, (chunk + PER_PLANE) % chunks)
                total = apply_link(links, chunk, spatial, False, ahead, total)
                behind = moved(
                    read, chunk, spatial, -1, (chunk - PER_PLANE + chunks) % chunks
                )
                total = apply_link(back, chunk, spatial, True, behind, total)
            for comp in range(6):
                if previous is None:
                    target[chunk, comp] = HOP_SCALE * total[comp]
                else:
                    target[chunk, comp] = (
                        2.0 * HOP_SCALE * total[comp] - previous[chunk, comp]
                    )

    buffers = [field, first, second]
    hop(field, None, first)
    for order in range(1, ITERS):
        hop(buffers[1], buffers[0], buffers[2])
        buffers = [buffers[1], buffers[2], buffers[0]]
    for index in range(count):
        outs[index][...] = buffers[1][index * slab : (index + 1) * slab]


def split(value):
    high = value.astype(jnp.bfloat16)
    low = (value - high.astype(jnp.float32)).astype(jnp.bfloat16)
    return high, low


def displace_kernel(me_ref, dirs_ref, cols_ref, links_ref, back_ref, out_ref):
    chunks, disps = out_ref.shape[0], out_ref.shape[1]
    tiles, size = cols_ref.shape[0], cols_ref.shape[3]
    unrolled = min(tiles, 4)
    for disp in range(disps):
        for heading in range(6):
            @pl.when(dirs_ref[disp] == heading)
            def _(disp=disp, heading=heading):
                spatial = heading % 3
                step = 1 if heading < 3 else -1
                table = links_ref if step > 0 else back_ref

                @pl.loop(0, chunks * (tiles // unrolled))
                def _(index):
                    chunk = index % chunks
                    results = []
                    for inner in range(unrolled):
                        turn = index // chunks * unrolled + inner
                        part = lambda where, comp: cols_ref[turn, where + PER_PLANE, comp]
                        source = moved(part, chunk, spatial, step, chunk + step * PER_PLANE)
                        total = apply_link(table, chunk, spatial, step < 0, source, [None] * 6)
                        results.append((turn, total))
                    for turn, total in results:
                        home = pl.multiple_of((me_ref[0] - turn + tiles) % tiles * size, size)
                        for comp in range(6):
                            out_ref[chunk, disp, comp, pl.ds(home, size), :] = total[comp]


def contract_kernel(spans, me_ref, *refs):
    rows_refs, refs = refs[:spans], refs[spans:]
    shifted_ref, cos_ref, sin_ref, out_ref, *scratch = refs
    staged, left_hi, left_lo, right_hi, right_lo = scratch
    shifted = shifted_ref.at[0]
    chunk = pl.program_id(0)
    disps = shifted_ref.shape[1]
    columns = shifted_ref.shape[3]
    row_count = staged.shape[1]
    momenta = cos_ref.shape[1]
    tiles, size = sum(ref.shape[1] for ref in rows_refs), rows_refs[0].shape[4]

    first = 0
    for rows_ref in rows_refs:

        @pl.loop(0, rows_ref.shape[1])
        def _(turn, rows_ref=rows_ref, first=first):
            home = (me_ref[0] - first - turn + tiles) % tiles * size
            for piece in range(rows_ref.shape[0]):
                place = pl.multiple_of(home + piece * columns, size)
                for comp in range(6):
                    staged[comp, pl.ds(place, size), :] = rows_ref[piece, turn, 0, comp]

        first += rows_ref.shape[1]

    for colour in range(3):
        real_at = pl.ds(2 * colour * LANES, LANES)
        imag_at = pl.ds((2 * colour + 1) * LANES, LANES)
        hi, lo = split(staged[colour])
        hi_i, lo_i = split(staged[3 + colour])
        for half, store_r, store_i in ((left_hi, hi, hi_i), (left_lo, lo, lo_i)):
            half[0:row_count, real_at] = store_r
            half[0:row_count, imag_at] = store_i
            half[row_count : 2 * row_count, real_at] = -store_i
            half[row_count : 2 * row_count, imag_at] = store_r
        for disp in range(disps):
            dr = shifted[disp, colour]
            di = shifted[disp, 3 + colour]
            for p in range(momenta):
                c = cos_ref[0, p : p + 1, :]
                s = sin_ref[0, p : p + 1, :]
                at = pl.ds((p * disps + disp) * columns, columns)
                hi, lo = split(c * dr + s * di)
                right_hi[at, real_at] = hi
                right_lo[at, real_at] = lo
                hi, lo = split(c * di - s * dr)
                right_hi[at, imag_at] = hi
                right_lo[at, imag_at] = lo

    @pl.when(chunk == 0)
    def _():
        out_ref[...] = jnp.zeros_like(out_ref)

    dims = (((1,), (1,)), ((), ()))
    dot = functools.partial(
        lax.dot_general, dimension_numbers=dims, preferred_element_type=jnp.float32
    )
    width = min(256, right_hi.shape[0])

    @pl.loop(0, right_hi.shape[0] // width)
    def _(block):
        at = pl.ds(pl.multiple_of(block * width, width), width)
        rh, rl = right_hi[at, :], right_lo[at, :]
        out_ref[:, at] += (
            dot(left_hi[...], rl) + dot(left_lo[...], rh) + dot(left_hi[...], rh)
        )


def phases(momenta, flat_index, extent_x):
    coord_x = flat_index // PLANE
    coord_y = flat_index % PLANE // LZ
    coord_z = flat_index % LZ
    part_x = jnp.mod(momenta[:, 0:1] * coord_x[None], extent_x).astype(jnp.float32) / extent_x
    part_y = jnp.mod(momenta[:, 1:2] * coord_y[None], LY).astype(jnp.float32) / LY
    part_z = jnp.mod(momenta[:, 2:3] * coord_z[None], LZ).astype(jnp.float32) / LZ
    angle = 2.0 * math.pi * (part_x + part_y + part_z)
    return (jnp.cos(angle), jnp.sin(angle))


def local(vectors, links, momenta, directions):
    nv = vectors.shape[1]
    sites = vectors.shape[3]
    tiles = lax.axis_size("tile")
    disps = directions.shape[0]
    moms = momenta.shape[0]
    chunks = sites // LANES
    every = chunks * tiles
    share = nv // tiles
    norm = 1.0 / math.sqrt(3.0 * sites * tiles)
    me = lax.axis_index("tile")
    here = me.reshape(1).astype(jnp.int32)
    groups, size = 1, share

    def passed(value, steps):
        if steps % tiles == 0:
            return value
        return lax.ppermute(value, "tile", [(i, (i + steps) % tiles) for i in range(tiles)])

    own_links = links.reshape(3, 18, chunks, LANES).transpose(2, 0, 1, 3)
    quarters = math.gcd(lax.axis_size("vec"), chunks)
    some_chunks = chunks // quarters
    mine_at = lax.axis_index("vec") % quarters * some_chunks
    quarter = lax.dynamic_slice_in_dim(own_links, mine_at, some_chunks, 0)
    quarter = lax.all_gather(quarter, "tile", axis=0)
    field = vectors.reshape(2, tiles, groups, size, 3, chunks, LANES)
    field = field.transpose(2, 1, 5, 0, 4, 3, 6)
    field = field.reshape(groups, tiles, chunks, 6, size, LANES)

    vmem = pl.BlockSpec(memory_space=pltpu.VMEM)
    smem = pl.BlockSpec(memory_space=pltpu.SMEM)
    piece = jax.ShapeDtypeStruct((chunks, 6, size, LANES), jnp.float32)
    whole_field = pltpu.VMEM((every, 6, size, LANES), jnp.float32)
    whole_links = pltpu.VMEM((every, 3, 18, LANES), jnp.float32)
    run_filter = pl.pallas_call(
        functools.partial(filter_kernel, tiles),
        out_shape=(piece,) * tiles + (jax.ShapeDtypeStruct(own_links.shape, jnp.float32),),
        in_specs=[smem] + [vmem] * (tiles + 1),
        out_specs=(vmem,) * (tiles + 1),
        scratch_shapes=[whole_field] * 3 + [whole_links] * 2,
        compiler_params=pltpu.CompilerParams(vmem_limit_bytes=VMEM_LIMIT),
        cost_estimate=pl.CostEstimate(
            flops=12 * 10**9, bytes_accessed=2 * 10**6, transcendentals=0
        ),
        name="filter",
    )
    rolled = jnp.stack(
        [lax.dynamic_index_in_dim(field, (me + turn) % tiles, 1, False) for turn in range(tiles)]
    )
    slabs, gathered, own_back = [], [], None
    rolled, quarter = lax.optimization_barrier((rolled, quarter))
    all_links = lax.all_gather(quarter, "vec", axis=0)[:quarters]
    all_links = all_links.transpose(1, 0, 2, 3, 4, 5).reshape(every, 3, 18, LANES)
    received = [
        [passed(rolled[turn, group], turn) for turn in range(tiles)] for group in range(groups)
    ]
    for group in range(groups):
        ordered = [received[group][(tiles - turn) % tiles] for turn in range(tiles)]
        *done, own_back = run_filter(here, *ordered, all_links)
        returned = [passed(done[turn], turn) for turn in range(tiles)]
        slabs.append(jnp.stack(returned))
        spans = [range(0, 1), range(1, 2), range(2, tiles)]
        for span in spans:
            part = jnp.stack([returned[turn] for turn in span])
            gathered.append(lax.all_gather(part, "vec", axis=0))

    def halo(value, heading, steps):
        return lax.cond(
            jnp.any(directions == heading), lambda x: passed(x, steps), lambda x: x, value
        )

    wide = []
    for slab in slabs:
        before = halo(slab[:, chunks - PER_PLANE :], 3, 1)
        after = halo(slab[:, :PER_PLANE], 0, -1)
        wide.append((before, slab, after))
    for group, (before, slab, after) in enumerate(wide):
        before = jnp.roll(before, 1, axis=0)
        after = jnp.roll(after, -1, axis=0)
        wide[group] = jnp.concatenate([before, slab, after], axis=1)

    flat_index = me * sites + jnp.arange(sites, dtype=jnp.int32)
    cosine, sine = phases(momenta, flat_index, sites * tiles // PLANE)
    cosine = (cosine * norm).reshape(moms, chunks, LANES).transpose(1, 0, 2)
    sine = (sine * norm).reshape(moms, chunks, LANES).transpose(1, 0, 2)

    row_count = nv * lax.axis_size("vec")
    halves = 2
    some = moms // halves
    width = some * disps * nv
    depth = 6 * LANES
    one = lambda shape: pl.BlockSpec((1,) + shape, lambda i: (i,) + (0,) * len(shape))
    row_blocks = [
        pl.BlockSpec(
            (row_count // nv, len(span), 1, 6, size, LANES), lambda i: (0, 0, i, 0, 0, 0)
        )
        for span in spans
    ]
    displaced = pl.pallas_call(
        displace_kernel,
        out_shape=jax.ShapeDtypeStruct((chunks, disps, 6, nv, LANES), jnp.float32),
        in_specs=[smem, smem, vmem, vmem, vmem],
        out_specs=vmem,
        compiler_params=pltpu.CompilerParams(vmem_limit_bytes=VMEM_LIMIT),
        name="displace",
    )(here, directions, wide[0], own_links, own_back)
    parts = []
    for half in range(halves):
        pick = slice(half * some, (half + 1) * some)
        partial = pl.pallas_call(
            functools.partial(contract_kernel, len(spans)),
            grid=(chunks,),
            out_shape=jax.ShapeDtypeStruct((2 * row_count, width), jnp.float32),
            in_specs=[
                smem,
                *row_blocks,
                one((disps, 6, nv, LANES)),
                one((some, LANES)),
                one((some, LANES)),
            ],
            out_specs=pl.BlockSpec((2 * row_count, width), lambda i: (0, 0)),
            scratch_shapes=[
                pltpu.VMEM((6, row_count, LANES), jnp.float32),
                pltpu.VMEM((2 * row_count, depth), jnp.bfloat16),
                pltpu.VMEM((2 * row_count, depth), jnp.bfloat16),
                pltpu.VMEM((width, depth), jnp.bfloat16),
                pltpu.VMEM((width, depth), jnp.bfloat16),
            ],
            compiler_params=pltpu.CompilerParams(vmem_limit_bytes=VMEM_LIMIT),
            cost_estimate=pl.CostEstimate(
                flops=20 * 10**9, bytes_accessed=12 * 10**6, transcendentals=0
            ),
            name="contract",
        )(here, *gathered, displaced, cosine[:, pick], sine[:, pick])
        partial = partial.reshape(2, row_count, width)
        mine = lax.psum_scatter(partial, "tile", scatter_dimension=1, tiled=True)
        parts.append(mine.reshape(2, row_count // tiles, some, disps, nv))
    mine = jnp.concatenate(parts, axis=2)
    return mine.transpose(1, 3, 0, 2, 4)


def solution(mesh):
    return jax.shard_map(
        local,
        mesh=mesh,
        in_specs=(
            P(None, "vec", None, ("groups", "tile")),
            P(None, None, None, None, ("groups", "tile")),
            P(),
            P(),
        ),
        out_specs=P(("groups", "tile"), None, None, None, "vec"),
        check_vma=False,
    )
```

```python
import functools
import math

import jax
import jax.numpy as jnp
from jax import lax
from jax.experimental import pallas as pl
from jax.experimental.pallas import tpu as pltpu
from jax.sharding import PartitionSpec as P

LY = 16
LZ = 32
ITERS = 4
PLANE = LY * LZ
LANES = 128
PER_PLANE = PLANE // LANES
HOP_SCALE = 0.125
VMEM_LIMIT = 60 * 1024 * 1024


def lane_index(like):
    return lax.broadcasted_iota(jnp.int32, like.shape, len(like.shape) - 1)


def shift_z(value, step):
    axis = len(value.shape) - 1
    lane = lane_index(value) % LZ
    if step > 0:
        plain = pltpu.roll(value, LANES - 1, axis)
        wrapped = pltpu.roll(value, LZ - 1, axis)
        return jnp.where(lane == LZ - 1, wrapped, plain)
    plain = pltpu.roll(value, 1, axis)
    wrapped = pltpu.roll(value, LANES - LZ + 1, axis)
    return jnp.where(lane == 0, wrapped, plain)


def shift_y(value, other, step):
    axis = len(value.shape) - 1
    lane = lane_index(value)
    if step > 0:
        return pltpu.roll(jnp.where(lane < LZ, other, value), LANES - LZ, axis)
    return pltpu.roll(jnp.where(lane >= LANES - LZ, other, value), LZ, axis)


def in_plane(chunk, step):
    base = chunk // PER_PLANE * PER_PLANE
    return base + (chunk + step + PER_PLANE) % PER_PLANE


def link_row(links, chunk, spatial, part, row, column):
    index = (part * 3 + row) * 3 + column
    return links[chunk, spatial, index : index + 1, :]


def apply_link(links, chunk, spatial, dagger, field, total):
    for row in range(3):
        real, imag = total[row], total[3 + row]
        for column in range(3):
            a, b = (column, row) if dagger else (row, column)
            lr = link_row(links, chunk, spatial, 0, a, b)
            li = link_row(links, chunk, spatial, 1, a, b)
            vr, vi = field[column], field[3 + column]
            if dagger:
                dr = lr * vr + li * vi
                di = lr * vi - li * vr
            else:
                dr = lr * vr - li * vi
                di = lr * vi + li * vr
            real = dr if real is None else real + dr
            imag = di if imag is None else imag + di
        total[row], total[3 + row] = real, imag
    return total


def moved(read, chunk, spatial, step, ahead_x):
    if spatial == 0:
        return [read(ahead_x, comp) for comp in range(6)]
    if spatial == 1:
        other = in_plane(chunk, step)
        return [shift_y(read(chunk, comp), read(other, comp), step) for comp in range(6)]
    return [shift_z(read(chunk, comp), step) for comp in range(6)]


def filter_kernel(count, me_ref, *refs):
    pieces, refs = refs[:count], refs[count:]
    all_links = refs[0]
    outs, refs = refs[1 : 1 + count], refs[1 + count :]
    own_back, field, first, second, links, back = refs
    chunks = field.shape[0]
    slab = chunks // count

    for index in range(count):
        field[index * slab : (index + 1) * slab] = pieces[index][...]

    @pl.loop(0, chunks)
    def _(chunk):
        links[chunk] = all_links[chunk]

    @pl.loop(0, chunks)
    def _(chunk):
        back[chunk, 0] = links[(chunk - PER_PLANE + chunks) % chunks, 0]
        back[chunk, 1] = shift_y(links[chunk, 1], links[in_plane(chunk, -1), 1], -1)
        back[chunk, 2] = shift_z(links[chunk, 2], -1)

    own_back[...] = back[0:slab]

    def hop(source, previous, target):
        @pl.loop(0, chunks)
        def _(chunk):
            read = lambda at, comp: source[at, comp]
            total = [None] * 6
            for spatial in range(3):
                ahead = moved(read, chunk, spatial, 1, (chunk + PER_PLANE) % chunks)
                total = apply_link(links, chunk, spatial, False, ahead, total)
                behind = moved(
                    read, chunk, spatial, -1, (chunk - PER_PLANE + chunks) % chunks
                )
                total = apply_link(back, chunk, spatial, True, behind, total)
            for comp in range(6):
                if previous is None:
                    target[chunk, comp] = HOP_SCALE * total[comp]
                else:
                    target[chunk, comp] = (
                        2.0 * HOP_SCALE * total[comp] - previous[chunk, comp]
                    )

    buffers = [field, first, second]
    hop(field, None, first)
    for order in range(1, ITERS):
        hop(buffers[1], buffers[0], buffers[2])
        buffers = [buffers[1], buffers[2], buffers[0]]
    for index in range(count):
        outs[index][...] = buffers[1][index * slab : (index + 1) * slab]


def split(value):
    high = value.astype(jnp.bfloat16)
    low = (value - high.astype(jnp.float32)).astype(jnp.bfloat16)
    return high, low


def displace_kernel(me_ref, dirs_ref, cols_ref, links_ref, back_ref, out_ref):
    chunks, disps = out_ref.shape[0], out_ref.shape[1]
    tiles, size = cols_ref.shape[0], cols_ref.shape[3]
    unrolled = min(tiles, 4)
    for disp in range(disps):
        for heading in range(6):
            @pl.when(dirs_ref[disp] == heading)
            def _(disp=disp, heading=heading):
                spatial = heading % 3
                step = 1 if heading < 3 else -1
                table = links_ref if step > 0 else back_ref

                @pl.loop(0, chunks * (tiles // unrolled))
                def _(index):
                    chunk = index % chunks
                    results = []
                    for inner in range(unrolled):
                        turn = index // chunks * unrolled + inner
                        part = lambda where, comp: cols_ref[turn, where + PER_PLANE, comp]
                        source = moved(part, chunk, spatial, step, chunk + step * PER_PLANE)
                        total = apply_link(table, chunk, spatial, step < 0, source, [None] * 6)
                        results.append((turn, total))
                    for turn, total in results:
                        home = pl.multiple_of((me_ref[0] - turn + tiles) % tiles * size, size)
                        for comp in range(6):
                            out_ref[chunk, disp, comp, pl.ds(home, size), :] = total[comp]


def contract_kernel(spans, me_ref, *refs):
    rows_refs, refs = refs[:spans], refs[spans:]
    shifted_ref, cos_ref, sin_ref, out_ref, *scratch = refs
    staged, left_hi, left_lo, right_hi, right_lo = scratch
    shifted = shifted_ref.at[0]
    chunk = pl.program_id(0)
    disps = shifted_ref.shape[1]
    columns = shifted_ref.shape[3]
    row_count = staged.shape[1]
    momenta = cos_ref.shape[1]
    tiles, size = sum(ref.shape[1] for ref in rows_refs), rows_refs[0].shape[4]

    first = 0
    for rows_ref in rows_refs:

        @pl.loop(0, rows_ref.shape[1])
        def _(turn, rows_ref=rows_ref, first=first):
            home = (me_ref[0] - first - turn + tiles) % tiles * size
            for piece in range(rows_ref.shape[0]):
                place = pl.multiple_of(home + piece * columns, size)
                for comp in range(6):
                    staged[comp, pl.ds(place, size), :] = rows_ref[piece, turn, 0, comp]

        first += rows_ref.shape[1]

    for colour in range(3):
        real_at = pl.ds(2 * colour * LANES, LANES)
        imag_at = pl.ds((2 * colour + 1) * LANES, LANES)
        hi, lo = split(staged[colour])
        hi_i, lo_i = split(staged[3 + colour])
        for half, store_r, store_i in ((left_hi, hi, hi_i), (left_lo, lo, lo_i)):
            half[0:row_count, real_at] = store_r
            half[0:row_count, imag_at] = store_i
            half[row_count : 2 * row_count, real_at] = -store_i
            half[row_count : 2 * row_count, imag_at] = store_r
        for disp in range(disps):
            dr = shifted[disp, colour]
            di = shifted[disp, 3 + colour]
            for p in range(momenta):
                c = cos_ref[0, p : p + 1, :]
                s = sin_ref[0, p : p + 1, :]
                at = pl.ds((p * disps + disp) * columns, columns)
                hi, lo = split(c * dr + s * di)
                right_hi[at, real_at] = hi
                right_lo[at, real_at] = lo
                hi, lo = split(c * di - s * dr)
                right_hi[at, imag_at] = hi
                right_lo[at, imag_at] = lo

    @pl.when(chunk == 0)
    def _():
        out_ref[...] = jnp.zeros_like(out_ref)

    dims = (((1,), (1,)), ((), ()))
    dot = functools.partial(
        lax.dot_general, dimension_numbers=dims, preferred_element_type=jnp.float32
    )
    width = min(256, right_hi.shape[0])

    @pl.loop(0, right_hi.shape[0] // width)
    def _(block):
        at = pl.ds(pl.multiple_of(block * width, width), width)
        rh, rl = right_hi[at, :], right_lo[at, :]
        out_ref[:, at] += (
            dot(left_hi[...], rl) + dot(left_lo[...], rh) + dot(left_hi[...], rh)
        )


def phases(momenta, flat_index, extent_x):
    coord_x = flat_index // PLANE
    coord_y = flat_index % PLANE // LZ
    coord_z = flat_index % LZ
    part_x = jnp.mod(momenta[:, 0:1] * coord_x[None], extent_x).astype(jnp.float32) / extent_x
    part_y = jnp.mod(momenta[:, 1:2] * coord_y[None], LY).astype(jnp.float32) / LY
    part_z = jnp.mod(momenta[:, 2:3] * coord_z[None], LZ).astype(jnp.float32) / LZ
    angle = 2.0 * math.pi * (part_x + part_y + part_z)
    return (jnp.cos(angle), jnp.sin(angle))


def local(vectors, links, momenta, directions):
    nv = vectors.shape[1]
    sites = vectors.shape[3]
    tiles = lax.axis_size("tile")
    disps = directions.shape[0]
    moms = momenta.shape[0]
    chunks = sites // LANES
    every = chunks * tiles
    share = nv // tiles
    norm = 1.0 / math.sqrt(3.0 * sites * tiles)
    me = lax.axis_index("tile")
    here = me.reshape(1).astype(jnp.int32)
    groups, size = 1, share

    def passed(value, steps):
        if steps % tiles == 0:
            return value
        return lax.ppermute(value, "tile", [(i, (i + steps) % tiles) for i in range(tiles)])

    own_links = links.reshape(3, 18, chunks, LANES).transpose(2, 0, 1, 3)
    quarters = math.gcd(lax.axis_size("vec"), chunks)
    some_chunks = chunks // quarters
    mine_at = lax.axis_index("vec") % quarters * some_chunks
    quarter = lax.dynamic_slice_in_dim(own_links, mine_at, some_chunks, 0)
    quarter = jnp.stack([passed(quarter, -turn) for turn in range(tiles)])
    field = vectors.reshape(2, tiles, groups, size, 3, chunks, LANES)
    field = field.transpose(2, 1, 5, 0, 4, 3, 6)
    field = field.reshape(groups, tiles, chunks, 6, size, LANES)

    vmem = pl.BlockSpec(memory_space=pltpu.VMEM)
    smem = pl.BlockSpec(memory_space=pltpu.SMEM)
    piece = jax.ShapeDtypeStruct((chunks, 6, size, LANES), jnp.float32)
    whole_field = pltpu.VMEM((every, 6, size, LANES), jnp.float32)
    whole_links = pltpu.VMEM((every, 3, 18, LANES), jnp.float32)
    run_filter = pl.pallas_call(
        functools.partial(filter_kernel, tiles),
        out_shape=(piece,) * tiles + (jax.ShapeDtypeStruct(own_links.shape, jnp.float32),),
        in_specs=[smem] + [vmem] * (tiles + 1),
        out_specs=(vmem,) * (tiles + 1),
        scratch_shapes=[whole_field] * 3 + [whole_links] * 2,
        compiler_params=pltpu.CompilerParams(vmem_limit_bytes=VMEM_LIMIT),
        cost_estimate=pl.CostEstimate(
            flops=12 * 10**9, bytes_accessed=2 * 10**6, transcendentals=0
        ),
        name="filter",
    )
    rolled = jnp.stack(
        [lax.dynamic_index_in_dim(field, (me + turn) % tiles, 1, False) for turn in range(tiles)]
    )
    slabs, gathered, own_back = [], [], None
    rolled, quarter = lax.optimization_barrier((rolled, quarter))
    all_links = lax.all_gather(quarter, "vec", axis=0)[:quarters]
    all_links = all_links.transpose(1, 0, 2, 3, 4, 5).reshape(every, 3, 18, LANES)
    received = [
        [passed(rolled[turn, group], turn) for turn in range(tiles)] for group in range(groups)
    ]
    for group in range(groups):
        ordered = [received[group][(tiles - turn) % tiles] for turn in range(tiles)]
        *done, own_back = run_filter(here, *ordered, all_links)
        returned = [passed(done[turn], turn) for turn in range(tiles)]
        slabs.append(jnp.stack(returned))
        spans = [range(0, 1), range(1, 2), range(2, tiles)]
        for span in spans:
            part = jnp.stack([returned[turn] for turn in span])
            gathered.append(lax.all_gather(part, "vec", axis=0))

    def halo(value, heading, steps):
        return lax.cond(
            jnp.any(directions == heading), lambda x: passed(x, steps), lambda x: x, value
        )

    wide = []
    for slab in slabs:
        before = halo(slab[:, chunks - PER_PLANE :], 3, 1)
        after = halo(slab[:, :PER_PLANE], 0, -1)
        wide.append((before, slab, after))
    for group, (before, slab, after) in enumerate(wide):
        before = jnp.roll(before, 1, axis=0)
        after = jnp.roll(after, -1, axis=0)
        wide[group] = jnp.concatenate([before, slab, after], axis=1)

    flat_index = me * sites + jnp.arange(sites, dtype=jnp.int32)
    cosine, sine = phases(momenta, flat_index, sites * tiles // PLANE)
    cosine = (cosine * norm).reshape(moms, chunks, LANES).transpose(1, 0, 2)
    sine = (sine * norm).reshape(moms, chunks, LANES).transpose(1, 0, 2)

    row_count = nv * lax.axis_size("vec")
    halves = 2
    some = moms // halves
    width = some * disps * nv
    depth = 6 * LANES
    one = lambda shape: pl.BlockSpec((1,) + shape, lambda i: (i,) + (0,) * len(shape))
    row_blocks = [
        pl.BlockSpec(
            (row_count // nv, len(span), 1, 6, size, LANES), lambda i: (0, 0, i, 0, 0, 0)
        )
        for span in spans
    ]
    displaced = pl.pallas_call(
        displace_kernel,
        out_shape=jax.ShapeDtypeStruct((chunks, disps, 6, nv, LANES), jnp.float32),
        in_specs=[smem, smem, vmem, vmem, vmem],
        out_specs=vmem,
        compiler_params=pltpu.CompilerParams(vmem_limit_bytes=VMEM_LIMIT),
        name="displace",
    )(here, directions, wide[0], own_links, own_back)
    parts = []
    for half in range(halves):
        pick = slice(half * some, (half + 1) * some)
        partial = pl.pallas_call(
            functools.partial(contract_kernel, len(spans)),
            grid=(chunks,),
            out_shape=jax.ShapeDtypeStruct((2 * row_count, width), jnp.float32),
            in_specs=[
                smem,
                *row_blocks,
                one((disps, 6, nv, LANES)),
                one((some, LANES)),
                one((some, LANES)),
            ],
            out_specs=pl.BlockSpec((2 * row_count, width), lambda i: (0, 0)),
            scratch_shapes=[
                pltpu.VMEM((6, row_count, LANES), jnp.float32),
                pltpu.VMEM((2 * row_count, depth), jnp.bfloat16),
                pltpu.VMEM((2 * row_count, depth), jnp.bfloat16),
                pltpu.VMEM((width, depth), jnp.bfloat16),
                pltpu.VMEM((width, depth), jnp.bfloat16),
            ],
            compiler_params=pltpu.CompilerParams(vmem_limit_bytes=VMEM_LIMIT),
            cost_estimate=pl.CostEstimate(
                flops=20 * 10**9, bytes_accessed=12 * 10**6, transcendentals=0
            ),
            name="contract",
        )(here, *gathered, displaced, cosine[:, pick], sine[:, pick])
        partial = partial.reshape(2, row_count, width)
        mine = lax.psum_scatter(partial, "tile", scatter_dimension=1, tiled=True)
        parts.append(mine.reshape(2, row_count // tiles, some, disps, nv))
    mine = jnp.concatenate(parts, axis=2)
    return mine.transpose(1, 3, 0, 2, 4)


def solution(mesh):
    return jax.shard_map(
        local,
        mesh=mesh,
        in_specs=(
            P(None, "vec", None, ("groups", "tile")),
            P(None, None, None, None, ("groups", "tile")),
            P(),
            P(),
        ),
        out_specs=P(("groups", "tile"), None, None, None, "vec"),
        check_vma=False,
    )
```
